32 devices in a mesh: dp: 4 (over z), row: 2 (over core), col: 4 (over y, x).
Axes of the slice: x: 2, y: 2, z: 4, core: 2. Of those that a mesh axis runs over, the one named last changes fastest.
Arguments:
- tokens: bfloat16 [4096, 2048], P(('dp', 'col'), 'row'), may hold values from -6 to 6
- norm1_gain: float32 [2048], replicated, may hold values from 0.25 to 1.75
- w_q: bfloat16 [2048, 2048], P('row', 'col'), may hold values from -0.125 to 0.125
- w_k: bfloat16 [2048, 1024], P('row', 'col'), may hold values from -0.125 to 0.125
- w_v: bfloat16 [2048, 1024], P('row', 'col'), may hold values from -0.125 to 0.125
- q_gain: float32 [128], replicated, may hold values from 0.5 to 3.5, as said below
- k_gain: float32 [128], replicated, may hold values from 0.5 to 3.5, as said below
- w_o: bfloat16 [2048, 2048], P('col', 'row'), may hold values from -0.75 to 0.75
- norm2_gain: float32 [2048], replicated, may hold values from 0.25 to 1.75
- w_gate: bfloat16 [2048, 6144], P('row', 'col'), may hold values from -0.125 to 0.125
- w_up: bfloat16 [2048, 6144], P('row', 'col'), may hold values from -0.125 to 0.125
- w_down: bfloat16 [6144, 2048], P('col', 'row'), may hold values from -0.078125 to 0.078125
- grad_out: bfloat16 [4096, 2048], P(('dp', 'col'), 'row'), may hold values from -6 to 6
Outputs:
- block_out: bfloat16 [4096, 2048], P(('dp', 'col'), 'row')
- grad_tokens: float32 [4096, 2048], P(('dp', 'col'), 'row')
- grad_norm1: float32 [2048], replicated
- grad_w_q: float32 [2048, 2048], P('row', 'col')
- grad_w_k: float32 [2048, 1024], P('row', 'col')
- grad_w_v: float32 [2048, 1024], P('row', 'col')
- grad_q_gain: float32 [128], replicated
- grad_k_gain: float32 [128], replicated
- grad_w_o: float32 [2048, 2048], P('col', 'row')
- grad_norm2: float32 [2048], replicated
- grad_w_gate: float32 [2048, 6144], P('row', 'col')
- grad_w_up: float32 [2048, 6144], P('row', 'col')
- grad_w_down: float32 [6144, 2048], P('col', 'row')
The draws below stay inside these ranges and needn't reach their ends.
Inputs may be any that keep to these rules, and one draw needn't show every extreme that they name: `q_gain`: positive. `k_gain`: positive.
All inputs are finite; a program needn't handle non-finite values.
Results may differ from the reference program's by a relative error of at most 0.0131.
The reference program's roundings to bfloat16 on the way count: a program that leaves them out, or rounds other values in their place, can miss the bound.
Values may be sent and summed in bfloat16 or wider, within the bound.
No kernel may reach another device: no remote copies, remote signals or barrier semaphores. Data moves between devices by JAX's collectives and lax.ppermute only.
A program may use at most 192 MiB of HBM per device.

```python
import math
import jax
import jax.numpy as jnp
from jax import lax

D = 2048
H = 16
KV = 8
HD = 128
FF = 6144
SEQ_LEN = 1024
TOKENS = 4096


def gain_draw(key, salt):
    sub_key = jax.random.fold_in(key, salt)
    return jnp.exp(jax.random.uniform(sub_key, (HD,), jnp.float32, math.log(0.5), math.log(2.0)))


def draw_q_gain(key, part):
    return gain_draw(key, 101)


def draw_k_gain(key, part):
    return gain_draw(key, 202)


def level_of(own_key, shape, split, least, top_value):
    level = 1.0
    for position, parts in split:
        heights = jax.random.uniform(jax.random.fold_in(jax.random.fold_in(own_key, 6), position), (parts,), jnp.float32, least / len(split), top_value / len(split))
        level = level * jnp.repeat(jnp.exp(heights), shape[position] // parts).reshape((-1,) + (1,) * (len(shape) - 1 - position))
    return level


def gaussian(stream_key, extent, scale, most, pieces=(), dtype=jnp.bfloat16):
    array = jax.random.normal(stream_key, extent, jnp.float32) * scale
    if len(pieces) > 0:
        array = level_of(stream_key, extent, pieces, -0.22, 0.18) * array
    return jnp.clip(array, min=-most, max=most).astype(dtype)


def setup_inputs(seed: int = 0) -> dict:
    streams_of = jax.random.split(jax.random.key(seed), 14)
    tokens = gaussian(streams_of[0], (TOKENS, D), 1.0, 6.0, ((0, 16), (1, 2)))
    norm1_gain = jnp.clip(1.0 + 0.15 * jax.random.normal(streams_of[1], (D,), jnp.float32), 0.25, 1.75)
    w_q = gaussian(streams_of[2], (D, H * HD), D ** -0.5, 0.125, ((0, 2), (1, 4)))
    w_k = gaussian(streams_of[3], (D, KV * HD), D ** -0.5, 0.125, ((0, 2), (1, 4)))
    w_v = gaussian(streams_of[4], (D, KV * HD), D ** -0.5, 0.125, ((0, 2), (1, 4)))
    q_gain = draw_q_gain(jax.random.fold_in(streams_of[13], 71), 0)
    k_gain = draw_k_gain(jax.random.fold_in(streams_of[13], 71), 0)
    w_o = gaussian(streams_of[7], (H * HD, D), (HD // 2) ** -0.5, 0.75, ((0, 4), (1, 2)))
    norm2_gain = jnp.clip(1.0 + 0.15 * jax.random.normal(streams_of[8], (D,), jnp.float32), 0.25, 1.75)
    w_gate = gaussian(streams_of[9], (D, FF), D ** -0.5, 0.125, ((0, 2), (1, 4)))
    w_up = gaussian(streams_of[10], (D, FF), D ** -0.5, 0.125, ((0, 2), (1, 4)))
    w_down = gaussian(streams_of[11], (FF, D), FF ** -0.5, 0.078125, ((0, 4), (1, 2)))
    grad_out = gaussian(streams_of[12], (TOKENS, D), 1.0, 6.0, ((0, 16), (1, 2)))
    return dict(tokens=tokens, norm1_gain=norm1_gain, w_q=w_q, w_k=w_k, w_v=w_v, q_gain=q_gain, k_gain=k_gain, w_o=w_o, norm2_gain=norm2_gain, w_gate=w_gate, w_up=w_up, w_down=w_down, grad_out=grad_out)


EPS = 1e-06
THETA = 1000000.0
NEGATIVE = -1e+30

def rope_tables():
    half_dim = HD // 2
    freqs = THETA ** (-(jnp.arange(half_dim).astype(jnp.float32) * (2.0 / HD)))
    angles = jnp.arange(SEQ_LEN).astype(jnp.float32)[:, None] * freqs[None, :]
    return (jnp.cos(angles)[:, None, :], jnp.sin(angles)[:, None, :])

def rotate(values, cosine, sine):
    half_dim = values.shape[-1] // 2
    first, second = (values[..., :half_dim], values[..., half_dim:])
    return jnp.concatenate([first * cosine - second * sine, second * cosine + first * sine], axis=-1)

def unrotate(grads, cosine, sine):
    half_dim = grads.shape[-1] // 2
    first, second = (grads[..., :half_dim], grads[..., half_dim:])
    return jnp.concatenate([first * cosine + second * sine, second * cosine - first * sine], axis=-1)

def head_norm(values, gain):
    inverse = lax.rsqrt(lax.optimization_barrier(jnp.mean(values * values, axis=-1, keepdims=True)) + EPS)
    return (values * inverse * gain, inverse)

def norm_back(values, inverse, gain, grads):
    unit_vals = values * inverse
    scaled = grads * gain
    inner = lax.optimization_barrier(jnp.mean(scaled * unit_vals, axis=-1, keepdims=True))
    return (inverse * (scaled - unit_vals * inner), grads * unit_vals)

def reference(tokens, norm1_gain, w_q, w_k, w_v, q_gain, k_gain, w_o, norm2_gain, w_gate, w_up, w_down, grad_out):
    heads_per = H // KV
    scale = HD ** (-0.5)
    cosine, sine = rope_tables()
    rows_at = jnp.arange(SEQ_LEN)[:, None]
    cols_at = jnp.arange(SEQ_LEN)[None, :]
    causal = cols_at <= rows_at

    def one_sequence(totals, pair):
        seq_tokens, seq_grad = pair
        inputs = seq_tokens.astype(jnp.float32)
        inverse_one = lax.rsqrt(lax.optimization_barrier(jnp.mean(inputs * inputs, axis=1, keepdims=True)) + EPS)
        normed_one = (inputs * inverse_one * norm1_gain).astype(jnp.bfloat16)
        query = jnp.dot(normed_one, w_q, preferred_element_type=jnp.float32).reshape(SEQ_LEN, H, HD)
        key_vals = jnp.dot(normed_one, w_k, preferred_element_type=jnp.float32).reshape(SEQ_LEN, KV, HD)
        value = jnp.dot(normed_one, w_v, preferred_element_type=jnp.float32).astype(jnp.bfloat16).reshape(SEQ_LEN, KV, HD)
        query_normed, query_inverse = head_norm(query, q_gain)
        key_normed, key_inverse = head_norm(key_vals, k_gain)
        query_rot = (rotate(query_normed, cosine, sine) * scale).astype(jnp.bfloat16).reshape(SEQ_LEN, KV, heads_per, HD)
        key_rot = rotate(key_normed, cosine, sine).astype(jnp.bfloat16)
        scores = jnp.einsum('qkgd,skd->kgqs', query_rot.astype(jnp.float32), key_rot.astype(jnp.float32))
        scores = jnp.where(causal, scores, NEGATIVE)
        row_top = lax.optimization_barrier(jnp.max(scores, axis=-1, keepdims=True))
        log_total = row_top + jnp.log(lax.optimization_barrier(jnp.sum(jnp.exp(scores - row_top), axis=-1, keepdims=True)))
        prob_full = jnp.exp(scores - log_total)
        probs = prob_full.astype(jnp.bfloat16)
        attn_heads = jnp.einsum('kgqs,skd->qkgd', probs.astype(jnp.float32), value.astype(jnp.float32))
        attn_heads = attn_heads.astype(jnp.bfloat16).reshape(SEQ_LEN, H * HD)
        mid = inputs + jnp.dot(attn_heads, w_o, preferred_element_type=jnp.float32)
        inverse_two = lax.rsqrt(lax.optimization_barrier(jnp.mean(mid * mid, axis=1, keepdims=True)) + EPS)
        normed_two = (mid * inverse_two * norm2_gain).astype(jnp.bfloat16)
        gate_vals = jnp.dot(normed_two, w_gate, preferred_element_type=jnp.float32)
        up_vals = jnp.dot(normed_two, w_up, preferred_element_type=jnp.float32)
        sigm = jax.nn.sigmoid(gate_vals)
        silu_vals = gate_vals * sigm
        hidden = (silu_vals * up_vals).astype(jnp.bfloat16)
        block_out = (mid + jnp.dot(hidden, w_down, preferred_element_type=jnp.float32)).astype(jnp.bfloat16)
        grad_w_down = jnp.dot(hidden.T, seq_grad, preferred_element_type=jnp.float32)
        grad_hidden = jnp.dot(seq_grad, w_down.T, preferred_element_type=jnp.float32)
        grad_gate = (grad_hidden * up_vals * sigm * (1.0 + gate_vals * (1.0 - sigm))).astype(jnp.bfloat16)
        grad_up = (grad_hidden * silu_vals).astype(jnp.bfloat16)
        grad_w_gate = jnp.dot(normed_two.T, grad_gate, preferred_element_type=jnp.float32)
        grad_w_up = jnp.dot(normed_two.T, grad_up, preferred_element_type=jnp.float32)
        grad_normed_two = jnp.dot(grad_gate, w_gate.T, preferred_element_type=jnp.float32) + jnp.dot(grad_up, w_up.T, preferred_element_type=jnp.float32)
        grad_mid_norm, gain_two_terms = norm_back(mid, inverse_two, norm2_gain, grad_normed_two)
        grad_mid = seq_grad.astype(jnp.float32) + grad_mid_norm
        grad_mid_low = grad_mid.astype(jnp.bfloat16)
        grad_w_o = jnp.dot(attn_heads.T, grad_mid_low, preferred_element_type=jnp.float32)
        grad_heads = jnp.dot(grad_mid_low, w_o.T, preferred_element_type=jnp.float32).astype(jnp.bfloat16)
        grad_heads = grad_heads.reshape(SEQ_LEN, KV, heads_per, HD)
        grad_value = jnp.einsum('kgqs,qkgd->skd', probs.astype(jnp.float32), grad_heads.astype(jnp.float32))
        grad_value = grad_value.astype(jnp.bfloat16).reshape(SEQ_LEN, KV * HD)
        grad_probs = jnp.einsum('qkgd,skd->kgqs', grad_heads.astype(jnp.float32), value.astype(jnp.float32))
        row_inner = lax.optimization_barrier(jnp.sum(prob_full * grad_probs, axis=-1, keepdims=True))
        grad_scores = (prob_full * (grad_probs - row_inner)).astype(jnp.bfloat16)
        grad_query_rot = jnp.einsum('kgqs,skd->qkgd', grad_scores.astype(jnp.float32), key_rot.astype(jnp.float32)).reshape(SEQ_LEN, H, HD)
        grad_key_rot = jnp.einsum('kgqs,qkgd->skd', grad_scores.astype(jnp.float32), query_rot.astype(jnp.float32))
        grad_query_normed = unrotate(grad_query_rot * scale, cosine, sine)
        grad_key_normed = unrotate(grad_key_rot, cosine, sine)
        grad_query, query_gain_terms = norm_back(query, query_inverse, q_gain, grad_query_normed)
        grad_key, key_gain_terms = norm_back(key_vals, key_inverse, k_gain, grad_key_normed)
        grad_query = grad_query.reshape(SEQ_LEN, H * HD).astype(jnp.bfloat16)
        grad_key = grad_key.reshape(SEQ_LEN, KV * HD).astype(jnp.bfloat16)
        grad_w_q = jnp.dot(normed_one.T, grad_query, preferred_element_type=jnp.float32)
        grad_w_k = jnp.dot(normed_one.T, grad_key, preferred_element_type=jnp.float32)
        grad_w_v = jnp.dot(normed_one.T, grad_value, preferred_element_type=jnp.float32)
        grad_normed_one = jnp.dot(grad_query, w_q.T, preferred_element_type=jnp.float32)
        grad_normed_one = grad_normed_one + jnp.dot(grad_key, w_k.T, preferred_element_type=jnp.float32)
        grad_normed_one = grad_normed_one + jnp.dot(grad_value, w_v.T, preferred_element_type=jnp.float32)
        grad_input_norm, gain_one_terms = norm_back(inputs, inverse_one, norm1_gain, grad_normed_one)
        grad_tokens = grad_mid + grad_input_norm
        terms = (lax.optimization_barrier(jnp.sum(gain_one_terms, axis=0)), grad_w_q, grad_w_k, grad_w_v, lax.optimization_barrier(jnp.sum(query_gain_terms, axis=(0, 1))), lax.optimization_barrier(jnp.sum(key_gain_terms, axis=(0, 1))), grad_w_o, lax.optimization_barrier(jnp.sum(gain_two_terms, axis=0)), grad_w_gate, grad_w_up, grad_w_down)
        return (jax.tree.map(jnp.add, totals, terms), (block_out, grad_tokens))
    start_totals = (jnp.zeros((D,), jnp.float32), jnp.zeros((D, H * HD), jnp.float32), jnp.zeros((D, KV * HD), jnp.float32), jnp.zeros((D, KV * HD), jnp.float32), jnp.zeros((HD,), jnp.float32), jnp.zeros((HD,), jnp.float32), jnp.zeros((H * HD, D), jnp.float32), jnp.zeros((D,), jnp.float32), jnp.zeros((D, FF), jnp.float32), jnp.zeros((D, FF), jnp.float32), jnp.zeros((FF, D), jnp.float32))
    seq_tokens_all = tokens.reshape(-1, SEQ_LEN, D)
    seq_grads_all = grad_out.reshape(-1, SEQ_LEN, D)
    totals, stacked = lax.scan(one_sequence, start_totals, (seq_tokens_all, seq_grads_all))
    block_out = stacked[0].reshape(-1, D)
    grad_tokens = stacked[1].reshape(-1, D)
    return (block_out, grad_tokens, totals[0], totals[1], totals[2], totals[3], totals[4], totals[5], totals[6], totals[7], totals[8], totals[9], totals[10])
```

```python
import jax
import jax.numpy as jnp
from jax import lax
from jax.sharding import PartitionSpec as P

SEQ_LEN = 1024


EPS = 1e-06
THETA = 1000000.0
NEGATIVE = -1e30
CONTRACT_ROWS = (((0,), (0,)), ((), ()))
CONTRACT_COLS = (((1,), (1,)), ((), ()))
F32 = jnp.float32
BF16 = jnp.bfloat16


def rows_product(left, right):
    return lax.dot_general(left, right, CONTRACT_ROWS, preferred_element_type=F32)


def cols_product(left, right):
    return lax.dot_general(left, right, CONTRACT_COLS, preferred_element_type=F32)


def plain_product(left, right):
    return jnp.dot(left, right, preferred_element_type=F32)


def take(values, index, size, axis):
    return lax.dynamic_slice_in_dim(values, index * size, size, axis)


def xor_hop(values, bit):
    count = lax.axis_size("col")
    return lax.ppermute(values, "col", [(i, i ^ bit) for i in range(count)])


def row_swap(values):
    return lax.ppermute(values, "row", [(0, 1), (1, 0)])


def row_sum(values):
    return values + row_swap(values)


def gather_tokens(values):
    if lax.axis_size("col") != 4:
        return [lax.all_gather(values, "col", axis=0, tiled=True)]
    half = values.shape[0] // 2
    by_one = xor_hop(values, 1)
    by_two = xor_hop(values, 2)
    low = xor_hop(by_two[:half], 1)
    high = xor_hop(by_one[half:], 2)
    return [values, by_one, by_two, low, high]


def scatter_tokens(values):
    if lax.axis_size("col") != 4:
        return lax.psum_scatter(values.astype(BF16), "col", scatter_dimension=0, tiled=True).astype(
            F32
        )
    rows = values.shape[0] // 4
    half = rows // 2
    low = BF16
    far_low = xor_hop(values[3 * rows : 3 * rows + half].astype(low), 1)
    far_high = xor_hop(values[3 * rows + half :].astype(low), 2)
    two_low = values[2 * rows : 2 * rows + half] + far_low.astype(F32)
    one_high = values[rows + half : 2 * rows] + far_high.astype(F32)
    to_two = jnp.concatenate([two_low, values[2 * rows + half : 3 * rows]], axis=0).astype(low)
    to_one = jnp.concatenate([values[rows : rows + half], one_high], axis=0).astype(low)
    from_two = xor_hop(to_two, 2)
    from_one = xor_hop(to_one, 1)
    return values[:rows] + from_one.astype(F32) + from_two.astype(F32)


def reorder(values, rows):
    count = lax.axis_size("col")
    if count != 4:
        return values
    me = lax.axis_index("col")
    parts = [take(values, me ^ place, rows, 0) for place in range(count)]
    return jnp.concatenate(parts, axis=0)


def line_total(parts):
    count = lax.axis_size("dp")
    if count != 4:
        return lax.psum(parts, "dp")
    inward = lax.ppermute(parts, "dp", [(0, 1), (3, 2)])
    pair = parts + inward
    across = lax.ppermute(pair, "dp", [(1, 2), (2, 1)])
    total = lax.optimization_barrier(pair + across)
    outward = lax.ppermute(total, "dp", [(1, 0), (2, 3)])
    place = lax.axis_index("dp")
    inner = (place == 1) | (place == 2)
    return jnp.where(inner, total, outward)


def rope_tables(seq_len, head_dim):
    half_dim = head_dim // 2
    freqs = THETA ** (-(jnp.arange(half_dim).astype(F32) * (2.0 / head_dim)))
    angles = jnp.arange(seq_len).astype(F32)[:, None] * freqs[None, :]
    return (jnp.cos(angles)[:, None, :], jnp.sin(angles)[:, None, :])


def rotate(values, cosine, sine):
    half_dim = values.shape[-1] // 2
    first, second = (values[..., :half_dim], values[..., half_dim:])
    return jnp.concatenate(
        [first * cosine - second * sine, second * cosine + first * sine], axis=-1
    )


def unrotate(grads, cosine, sine):
    half_dim = grads.shape[-1] // 2
    first, second = (grads[..., :half_dim], grads[..., half_dim:])
    return jnp.concatenate(
        [first * cosine + second * sine, second * cosine - first * sine], axis=-1
    )


def head_norm(values, gain):
    inverse = lax.rsqrt(jnp.mean(values * values, axis=-1, keepdims=True) + EPS)
    return (values * inverse * gain, inverse)


def head_back(values, inverse, gain, grads):
    unit_vals = values * inverse
    scaled = grads * gain
    inner = jnp.mean(scaled * unit_vals, axis=-1, keepdims=True)
    return (inverse * (scaled - unit_vals * inner), grads * unit_vals)


def rms_back(values, inverse, gain, grads, width):
    unit_vals = values * inverse
    scaled = grads * gain
    inner = row_sum(jnp.sum(scaled * unit_vals, axis=1)) / width
    return (inverse * (scaled - unit_vals * inner[:, None]), jnp.sum(grads * unit_vals, axis=0))


def block_scores(query_block, key_block, start):
    scores = jnp.einsum("qkgd,skd->kgqs", query_block, key_block, preferred_element_type=F32)
    rows_at = start + jnp.arange(query_block.shape[0])[:, None]
    cols_at = jnp.arange(key_block.shape[0])[None, :]
    return jnp.where(cols_at <= rows_at, scores, NEGATIVE)


def on_device(
    tokens,
    norm1_gain,
    w_q,
    w_k,
    w_v,
    q_gain,
    k_gain,
    w_o,
    norm2_gain,
    w_gate,
    w_up,
    w_down,
    grad_out,
):
    me = lax.axis_index("row")
    mate = 1 - me
    own_rows = tokens.shape[0]
    width_local = tokens.shape[1]
    width = width_local * lax.axis_size("row")
    gain_one = take(norm1_gain, me, width_local, 0)
    gain_one_mate = take(norm1_gain, mate, width_local, 0)
    gain_two = take(norm2_gain, me, width_local, 0)
    head_dim = q_gain.shape[0]
    scale = head_dim ** (-0.5)
    q_cols = w_q.shape[1] // 2
    k_cols = w_k.shape[1] // 2
    units = w_gate.shape[1] // 2

    tokens_mine = jnp.concatenate(gather_tokens(tokens), axis=0)
    tokens_mate = row_swap(tokens_mine)

    qkv_mine = jnp.concatenate(
        [take(w_q, me, q_cols, 1), take(w_k, me, k_cols, 1), take(w_v, me, k_cols, 1)], axis=1
    )
    qkv_away = jnp.concatenate(
        [take(w_q, mate, q_cols, 1), take(w_k, mate, k_cols, 1), take(w_v, mate, k_cols, 1)],
        axis=1,
    )
    qkv_mate = row_swap(qkv_away)
    gate_mine = take(w_gate, me, units, 1)
    gate_away = take(w_gate, mate, units, 1)
    gate_mate = row_swap(gate_away)
    up_mine = take(w_up, me, units, 1)
    up_away = take(w_up, mate, units, 1)
    up_mate = row_swap(up_away)
    down_mine = take(w_down, me, units, 0)
    down_away = take(w_down, mate, units, 0)
    down_mate = row_swap(down_away)

    part_mine = tokens_mine.astype(F32)
    part_mate = tokens_mate.astype(F32)
    square_sum = jnp.sum(part_mine * part_mine, axis=1) + jnp.sum(part_mate * part_mate, axis=1)
    inverse_full = lax.rsqrt(square_sum / width + EPS)[:, None]
    normed_mine = (part_mine * inverse_full * gain_one).astype(BF16)
    normed_mate = (part_mate * inverse_full * gain_one_mate).astype(BF16)
    qkv_full = plain_product(normed_mine, qkv_mine) + plain_product(normed_mate, qkv_mate)
    qkv_full = reorder(qkv_full, own_rows)
    group_rows = qkv_full.shape[0]
    q_heads = q_cols // head_dim
    kv_heads = k_cols // head_dim
    heads_per = q_heads // kv_heads
    block_rows = min(512, SEQ_LEN)
    block_count = SEQ_LEN // block_rows
    cosine, sine = rope_tables(SEQ_LEN, head_dim)
    query_three = qkv_full[:, :q_cols].reshape(group_rows, q_heads, head_dim)
    key_three = qkv_full[:, q_cols : q_cols + k_cols].reshape(group_rows, kv_heads, head_dim)
    query_normed, query_inverse = head_norm(query_three, q_gain)
    key_normed, key_inverse = head_norm(key_three, k_gain)
    query_rot = (rotate(query_normed, cosine, sine) * scale).astype(BF16)
    query_rot = query_rot.reshape(group_rows, kv_heads, heads_per, head_dim)
    key_rot = rotate(key_normed, cosine, sine).astype(BF16)
    value_three = qkv_full[:, q_cols + k_cols :].astype(BF16)
    value_three = value_three.reshape(group_rows, kv_heads, head_dim)
    out_blocks = []
    lse_blocks = []
    for block_index in range(block_count):
        start = block_index * block_rows
        finish = start + block_rows
        scores = block_scores(query_rot[start:finish], key_rot[:finish], start)
        row_top = jnp.max(scores, axis=-1, keepdims=True)
        log_total = row_top + jnp.log(jnp.sum(jnp.exp(scores - row_top), axis=-1, keepdims=True))
        probs = jnp.exp(scores - log_total).astype(BF16)
        out_vals = jnp.einsum(
            "kgqs,skd->qkgd", probs, value_three[:finish], preferred_element_type=F32
        )
        out_blocks.append(out_vals.astype(BF16).reshape(block_rows, q_cols))
        lse_blocks.append(log_total)
    heads_mine = reorder(jnp.concatenate(out_blocks, axis=0), own_rows)
    heads_mate = row_swap(heads_mine)
    o_mine = take(w_o, me, q_cols, 0)
    o_away = take(w_o, mate, q_cols, 0)
    attn_out = scatter_tokens(plain_product(heads_mine, o_mine) + plain_product(heads_mate, o_away))
    inputs = tokens.astype(F32)
    mid = inputs + attn_out
    inverse_two = lax.rsqrt(row_sum(jnp.sum(mid * mid, axis=1)) / width + EPS)[:, None]
    normed_two = (mid * inverse_two * gain_two).astype(BF16)
    two_mine = jnp.concatenate(gather_tokens(normed_two), axis=0)
    two_mate = row_swap(two_mine)

    grads_mine = jnp.concatenate(gather_tokens(grad_out), axis=0)
    grads_mate = row_swap(grads_mine)
    grad_hidden = cols_product(grads_mine, down_mine) + cols_product(grads_mate, down_mate)

    gate_vals = plain_product(two_mine, gate_mine) + plain_product(two_mate, gate_mate)
    up_vals = plain_product(two_mine, up_mine) + plain_product(two_mate, up_mate)
    sigm = jax.nn.sigmoid(gate_vals)
    silu_vals = gate_vals * sigm
    hidden_mine = (silu_vals * up_vals).astype(BF16)
    grad_gate = (grad_hidden * up_vals * sigm * (1.0 + gate_vals * (1.0 - sigm))).astype(BF16)
    grad_up = (grad_hidden * silu_vals).astype(BF16)
    hidden_mate = row_swap(hidden_mine)
    grad_gate_mate = row_swap(grad_gate)
    grad_up_mate = row_swap(grad_up)

    def weight_grad(left, right):
        return line_total(rows_product(left, right).astype(BF16))

    down_a = weight_grad(hidden_mine, grads_mine)
    gate_a = weight_grad(two_mine, grad_gate)
    up_a = weight_grad(two_mine, grad_up)
    down_b = weight_grad(hidden_mate, grads_mine)
    gate_b = weight_grad(two_mine, grad_gate_mate)
    up_b = weight_grad(two_mine, grad_up_mate)

    grad_two_part = (
        cols_product(grad_gate, gate_mine)
        + cols_product(grad_up, up_mine)
        + cols_product(grad_gate_mate, gate_away)
        + cols_product(grad_up_mate, up_away)
    )
    grad_normed_two = scatter_tokens(grad_two_part)
    grad_mid_norm, gain_two_part = rms_back(mid, inverse_two, gain_two, grad_normed_two, width)
    grad_mid = grad_out.astype(F32) + grad_mid_norm
    grad_mid_low = grad_mid.astype(BF16)
    attn_mine = jnp.concatenate(gather_tokens(grad_mid_low), axis=0)
    o_a = weight_grad(heads_mine, attn_mine)
    o_b = weight_grad(heads_mate, attn_mine)
    grad_heads = (
        cols_product(attn_mine, o_mine) + row_swap(cols_product(attn_mine, o_away))
    ).astype(BF16)
    mlp_out = scatter_tokens(
        plain_product(hidden_mine, down_mine) + plain_product(hidden_mate, down_away)
    )
    block_out = (mid + mlp_out).astype(BF16)

    grad_three = reorder(grad_heads, own_rows).reshape(group_rows, kv_heads, heads_per, head_dim)
    query_grads = []
    key_accum = jnp.zeros((SEQ_LEN, kv_heads, head_dim), F32)
    value_accum = jnp.zeros((SEQ_LEN, kv_heads, head_dim), F32)
    for block_index in range(block_count):
        start = block_index * block_rows
        finish = start + block_rows
        query_block = query_rot[start:finish]
        key_block = key_rot[:finish]
        value_block = value_three[:finish]
        grad_block = grad_three[start:finish]
        scores = block_scores(query_block, key_block, start)
        prob_full = jnp.exp(scores - lse_blocks[block_index])
        probs = prob_full.astype(BF16)
        value_accum = value_accum.at[:finish].add(
            jnp.einsum("kgqs,qkgd->skd", probs, grad_block, preferred_element_type=F32)
        )
        grad_probs = jnp.einsum(
            "qkgd,skd->kgqs", grad_block, value_block, preferred_element_type=F32
        )
        row_inner = jnp.sum(prob_full * grad_probs, axis=-1, keepdims=True)
        grad_scores = (prob_full * (grad_probs - row_inner)).astype(BF16)
        query_piece = jnp.einsum(
            "kgqs,skd->qkgd", grad_scores, key_block, preferred_element_type=F32
        )
        query_grads.append(query_piece.reshape(block_rows, q_heads, head_dim))
        key_accum = key_accum.at[:finish].add(
            jnp.einsum("kgqs,qkgd->skd", grad_scores, query_block, preferred_element_type=F32)
        )
    grad_query_rot = jnp.concatenate(query_grads, axis=0)
    grad_value = value_accum.astype(BF16).reshape(group_rows, k_cols)
    grad_query_normed = unrotate(grad_query_rot * scale, cosine, sine)
    grad_key_normed = unrotate(key_accum, cosine, sine)
    grad_query, query_gain_terms = head_back(query_three, query_inverse, q_gain, grad_query_normed)
    grad_key, key_gain_terms = head_back(key_three, key_inverse, k_gain, grad_key_normed)
    grad_query = grad_query.reshape(group_rows, q_cols).astype(BF16)
    grad_key = grad_key.reshape(group_rows, k_cols).astype(BF16)
    grad_qkv = reorder(jnp.concatenate([grad_query, grad_key, grad_value], axis=1), own_rows)
    grad_qkv_mate = row_swap(grad_qkv)
    qk_cols = q_cols + k_cols
    q_a = weight_grad(normed_mine, grad_qkv[:, :q_cols])
    q_b = weight_grad(normed_mine, grad_qkv_mate[:, :q_cols])
    kv_a = weight_grad(normed_mine, grad_qkv[:, q_cols:])
    kv_b = weight_grad(normed_mine, grad_qkv_mate[:, q_cols:])
    input_part = cols_product(grad_qkv, qkv_mine) + cols_product(grad_qkv_mate, qkv_away)
    grad_normed_one = scatter_tokens(input_part)
    inverse_one = inverse_full[:own_rows]
    if lax.axis_size("col") != 4:
        inverse_one = take(inverse_full, lax.axis_index("col"), own_rows, 0)
    grad_input_norm, gain_one_part = rms_back(inputs, inverse_one, gain_one, grad_normed_one, width)
    grad_tokens = grad_mid + grad_input_norm

    gains = [
        lax.dynamic_update_slice_in_dim(
            jnp.zeros((width,), F32), part, me * width_local, 0
        )
        for part in (gain_one_part, gain_two_part)
    ]
    gains.append(jnp.sum(query_gain_terms, axis=(0, 1)))
    gains.append(jnp.sum(key_gain_terms, axis=(0, 1)))
    gain_sum = row_sum(jnp.concatenate(gains))
    if lax.axis_size("col") == 4:
        gain_sum = gain_sum + xor_hop(gain_sum, 1)
        gain_sum = gain_sum + xor_hop(gain_sum, 2)
    else:
        gain_sum = lax.psum(gain_sum, "col")
    gain_sum = line_total(gain_sum)
    grad_norm1 = gain_sum[:width]
    grad_norm2 = gain_sum[width : 2 * width]
    grad_q_gain = gain_sum[2 * width : 2 * width + head_dim]
    grad_k_gain = gain_sum[2 * width + head_dim :]

    def place(first, second, axis):
        size = first.shape[axis]
        shape = list(first.shape)
        shape[axis] = 2 * size
        whole = jnp.zeros(shape, F32)
        whole = lax.dynamic_update_slice_in_dim(whole, first.astype(F32), me * size, axis)
        return lax.dynamic_update_slice_in_dim(whole, second.astype(F32), mate * size, axis)

    return (
        block_out,
        grad_tokens,
        grad_norm1,
        place(q_a, q_b, 1),
        place(kv_a[:, :k_cols], kv_b[:, :k_cols], 1),
        place(kv_a[:, k_cols:], kv_b[:, k_cols:], 1),
        grad_q_gain,
        grad_k_gain,
        place(o_a, o_b, 0),
        grad_norm2,
        place(gate_a, gate_b, 1),
        place(up_a, up_b, 1),
        place(down_a, down_b, 0),
    )


def solution(mesh):
    return jax.shard_map(
        on_device,
        mesh=mesh,
        in_specs=(
            P(("dp", "col"), "row"),
            P(),
            P("row", "col"),
            P("row", "col"),
            P("row", "col"),
            P(),
            P(),
            P("col", "row"),
            P(),
            P("row", "col"),
            P("row", "col"),
            P("col", "row"),
            P(("dp", "col"), "row"),
        ),
        out_specs=(
            P(("dp", "col"), "row"),
            P(("dp", "col"), "row"),
            P(),
            P("row", "col"),
            P("row", "col"),
            P("row", "col"),
            P(),
            P(),
            P("col", "row"),
            P(),
            P("row", "col"),
            P("row", "col"),
            P("col", "row"),
        ),
        check_vma=False,
    )
```

```python
import jax
import jax.numpy as jnp
from jax import lax
from jax.experimental import pallas as pl
from jax.experimental.pallas import tpu as pltpu
from jax.sharding import PartitionSpec as P


SEQ_LEN = 1024


EPS = 1e-06
THETA = 1000000.0
NEGATIVE = -1e30
CONTRACT_ROWS = (((0,), (0,)), ((), ()))
CONTRACT_COLS = (((1,), (1,)), ((), ()))
F32 = jnp.float32
BF16 = jnp.bfloat16


def rows_product(left, right):
    return lax.dot_general(left, right, CONTRACT_ROWS, preferred_element_type=F32)


def cols_product(left, right):
    return lax.dot_general(left, right, CONTRACT_COLS, preferred_element_type=F32)


def plain_product(left, right):
    return jnp.dot(left, right, preferred_element_type=F32)


def take(values, index, size, axis):
    return lax.dynamic_slice_in_dim(values, index * size, size, axis)


def xor_hop(values, bit):
    count = lax.axis_size("col")
    return lax.ppermute(values, "col", [(i, i ^ bit) for i in range(count)])


def row_swap(values):
    return lax.ppermute(values, "row", [(0, 1), (1, 0)])


def row_sum(values):
    return values + row_swap(values)


def gather_tokens(values, ahead=None):
    if lax.axis_size("col") != 4:
        blocks = [lax.all_gather(values, "col", axis=0, tiled=True)]
        return blocks if ahead is None else (blocks, ahead)
    half = values.shape[0] // 2
    by_one = xor_hop(values, 1)
    by_two = xor_hop(values, 2)
    if ahead is not None:
        by_one, by_two, ahead = lax.optimization_barrier((by_one, by_two, ahead))
    low = xor_hop(by_two[:half], 1)
    high = xor_hop(by_one[half:], 2)
    blocks = [values, by_one, by_two, low, high]
    return blocks if ahead is None else (blocks, ahead)


def scatter_tokens(values):
    if lax.axis_size("col") != 4:
        return lax.psum_scatter(values.astype(BF16), "col", scatter_dimension=0, tiled=True).astype(
            F32
        )
    rows = values.shape[0] // 4
    half = rows // 2
    low = BF16
    far_low = xor_hop(values[3 * rows : 3 * rows + half].astype(low), 1)
    far_high = xor_hop(values[3 * rows + half :].astype(low), 2)
    two_low = values[2 * rows : 2 * rows + half] + far_low.astype(F32)
    one_high = values[rows + half : 2 * rows] + far_high.astype(F32)
    to_two = jnp.concatenate([two_low, values[2 * rows + half : 3 * rows]], axis=0).astype(low)
    to_one = jnp.concatenate([values[rows : rows + half], one_high], axis=0).astype(low)
    from_two = xor_hop(to_two, 2)
    from_one = xor_hop(to_one, 1)
    return values[:rows] + from_one.astype(F32) + from_two.astype(F32)


class LineSums:
    def __init__(self):
        self.totals = {}
        spot = lax.axis_index("dp")
        self.inner = (spot == 1) | (spot == 2)

    def add(self, name, part):
        if lax.axis_size("dp") != 4:
            self.totals[name] = lax.psum(part, "dp")
            return
        inward = lax.ppermute(part, "dp", [(0, 1), (3, 2)])
        pair = part + inward
        across = lax.ppermute(pair, "dp", [(1, 2), (2, 1)])
        total = pair + across
        total = lax.optimization_barrier(total)
        outward = lax.ppermute(total, "dp", [(1, 0), (2, 3)])
        self.totals[name] = jnp.where(self.inner, total, outward)


def rope_tables(seq_len, head_dim):
    half_dim = head_dim // 2
    freqs = THETA ** (-(jnp.arange(half_dim).astype(F32) * (2.0 / head_dim)))
    angles = jnp.arange(seq_len).astype(F32)[:, None] * freqs[None, :]
    cosine, sine = jnp.cos(angles), jnp.sin(angles)
    return (
        jnp.concatenate([cosine, cosine], axis=1),
        jnp.concatenate([-sine, sine], axis=1),
    )


def turn(values, cosine, sine):
    return values * cosine + pltpu.roll(values, values.shape[1] // 2, 1) * sine


def head_inverse(values):
    return lax.rsqrt(jnp.mean(values * values, axis=1, keepdims=True) + EPS)


def head_back(values, gain, grads):
    inverse = head_inverse(values)
    unit_vals = values * inverse
    scaled = grads * gain
    inner = jnp.mean(scaled * unit_vals, axis=1, keepdims=True)
    terms = jnp.sum(grads * unit_vals, axis=0, keepdims=True)
    return (inverse * (scaled - unit_vals * inner), terms)


def call(kernel, grid, in_specs, out_specs, out_shape, scratch, flops, moved, *operands):
    return pl.pallas_call(
        kernel,
        out_shape=out_shape,
        grid_spec=pltpu.PrefetchScalarGridSpec(
            num_scalar_prefetch=1,
            grid=grid,
            in_specs=in_specs,
            out_specs=out_specs,
            scratch_shapes=scratch,
        ),
        compiler_params=pltpu.CompilerParams(
            dimension_semantics=("arbitrary",), vmem_limit_bytes=56 * 2**20
        ),
        cost_estimate=pl.CostEstimate(flops=flops, bytes_accessed=moved, transcendentals=0),
    )(*operands)


def whole(shape):
    return pl.BlockSpec(shape, lambda i, spots: (0,) * len(shape))


def project_qkv(spots, mine, mate, gain, gain_mate, w_mine, w_mate, q_gain, k_gain, cosine, sine):
    group_rows, width_local = mine.shape
    cols = w_mine.shape[1]
    head_dim = q_gain.shape[1]
    q_cols = cols // 2
    k_cols = cols // 4
    count = lax.axis_size("col")
    rows = group_rows // count
    width = 2 * width_local
    scale = head_dim ** (-0.5)

    def kernel(
        spots_ref, mine_ref, mate_ref, gain_ref, gain_mate_ref, w_ref, w_mate_ref, qg_ref, kg_ref,
        cos_ref, sin_ref, normed_ref, raw_ref, q_ref, k_ref, v_ref,
    ):
        left = mine_ref[...].astype(F32)
        right = mate_ref[...].astype(F32)
        squares = jnp.sum(left * left, axis=1, keepdims=True) + jnp.sum(
            right * right, axis=1, keepdims=True
        )
        inverse = lax.rsqrt(squares / width + EPS)
        normed = (left * inverse * gain_ref[...]).astype(BF16)
        normed_ref[...] = normed
        normed_mate = (right * inverse * gain_mate_ref[...]).astype(BF16)
        full = plain_product(normed, w_ref[...]) + plain_product(normed_mate, w_mate_ref[...])
        raw_ref[...] = full[:, : q_cols + k_cols]
        v_ref[...] = full[:, q_cols + k_cols :].astype(BF16)
        cosine_block, sine_block = cos_ref[...], sin_ref[...]
        for head in range(q_cols // head_dim):
            at = slice(head * head_dim, (head + 1) * head_dim)
            query = full[:, at]
            normal = query * head_inverse(query) * qg_ref[...]
            q_ref[:, at] = (turn(normal, cosine_block, sine_block) * scale).astype(BF16)
        for head in range(k_cols // head_dim):
            at = slice(head * head_dim, (head + 1) * head_dim)
            key = full[:, q_cols + head * head_dim : q_cols + (head + 1) * head_dim]
            normal = key * head_inverse(key) * kg_ref[...]
            k_ref[:, at] = turn(normal, cosine_block, sine_block).astype(BF16)

    def slot(i, spots):
        return (i ^ spots[0], 0)

    def straight(i, spots):
        return (i, 0)

    return call(
        kernel,
        (count,),
        [
            pl.BlockSpec((rows, width_local), slot),
            pl.BlockSpec((rows, width_local), slot),
            whole((1, width_local)),
            whole((1, width_local)),
            whole((width_local, cols)),
            whole((width_local, cols)),
            whole((1, head_dim)),
            whole((1, head_dim)),
            pl.BlockSpec((rows, head_dim), straight),
            pl.BlockSpec((rows, head_dim), straight),
        ],
        [
            pl.BlockSpec((rows, width_local), slot),
            pl.BlockSpec((rows, q_cols + k_cols), straight),
            pl.BlockSpec((rows, q_cols), straight),
            pl.BlockSpec((rows, k_cols), straight),
            pl.BlockSpec((rows, k_cols), straight),
        ],
        [
            jax.ShapeDtypeStruct((group_rows, width_local), BF16),
            jax.ShapeDtypeStruct((group_rows, q_cols + k_cols), F32),
            jax.ShapeDtypeStruct((group_rows, q_cols), BF16),
            jax.ShapeDtypeStruct((group_rows, k_cols), BF16),
            jax.ShapeDtypeStruct((group_rows, k_cols), BF16),
        ],
        [],
        4 * group_rows * width_local * cols,
        group_rows * width_local * 6 + width_local * cols * 4,
        spots, mine, mate, gain, gain_mate, w_mine, w_mate, q_gain, k_gain, cosine, sine,
    )


def stack_heads(values, kv_head, heads_per, head_dim):
    start = kv_head * heads_per
    return jnp.concatenate(
        [
            values[:, (start + h) * head_dim : (start + h + 1) * head_dim]
            for h in range(heads_per)
        ],
        axis=0,
    )


def causal(scores, rows):
    row = lax.broadcasted_iota(jnp.int32, scores.shape, 0) % rows
    col = lax.broadcasted_iota(jnp.int32, scores.shape, 1)
    return jnp.where(col <= row, scores, NEGATIVE)


def attend(spots, query, key, value, head_dim):
    group_rows, q_cols = query.shape
    k_cols = key.shape[1]
    kv_heads = k_cols // head_dim
    heads_per = q_cols // k_cols
    count = lax.axis_size("col")
    rows = group_rows // count

    def kernel(spots_ref, q_ref, k_ref, v_ref, out_ref, log_ref):
        step = pl.program_id(0)

        def block(index):
            start = index * rows
            for kv_head in range(kv_heads):
                at = slice(kv_head * head_dim, (kv_head + 1) * head_dim)
                queries = stack_heads(q_ref[...], kv_head, heads_per, head_dim)
                near = causal(cols_product(queries, k_ref[start : start + rows, at]), rows)
                top = jnp.max(near, axis=1, keepdims=True)
                if index:
                    far = cols_product(queries, k_ref[:start, at])
                    top = jnp.maximum(top, jnp.max(far, axis=1, keepdims=True))
                near = jnp.exp(near - top)
                total = jnp.sum(near, axis=1, keepdims=True)
                if index:
                    far = jnp.exp(far - top)
                    total = total + jnp.sum(far, axis=1, keepdims=True)
                share = 1.0 / total
                out = plain_product(
                    (near * share).astype(BF16), v_ref[start : start + rows, at]
                )
                if index:
                    out = out + plain_product((far * share).astype(BF16), v_ref[:start, at])
                for h in range(heads_per):
                    spot = (kv_head * heads_per + h) * head_dim
                    out_ref[:, spot : spot + head_dim] = out[h * rows : (h + 1) * rows].astype(
                        BF16
                    )
                log_ref[kv_head] = jnp.broadcast_to(
                    top + jnp.log(total), (heads_per * rows, head_dim)
                )

        for index in range(count):
            pl.when(step == index)(lambda index=index: block(index))

    return call(
        kernel,
        (count,),
        [
            pl.BlockSpec((rows, q_cols), lambda i, spots: (i, 0)),
            whole((group_rows, k_cols)),
            whole((group_rows, k_cols)),
        ],
        [
            pl.BlockSpec((rows, q_cols), lambda i, spots: (i ^ spots[0], 0)),
            pl.BlockSpec((kv_heads, heads_per * rows, head_dim), lambda i, spots: (0, i, 0)),
        ],
        [
            jax.ShapeDtypeStruct((group_rows, q_cols), BF16),
            jax.ShapeDtypeStruct((kv_heads, heads_per * group_rows, head_dim), F32),
        ],
        [],
        4 * group_rows * group_rows * q_cols,
        group_rows * q_cols * 12,
        spots, query, key, value,
    )


def attend_back(spots, query, key, value, logs, grads, raw, q_gain, k_gain, cosine, sine):
    group_rows, q_cols = query.shape
    k_cols = key.shape[1]
    head_dim = q_gain.shape[1]
    kv_heads = k_cols // head_dim
    heads_per = q_cols // k_cols
    count = lax.axis_size("col")
    rows = group_rows // count
    scale = head_dim ** (-0.5)

    def kernel(
        spots_ref, q_ref, k_ref, v_ref, log_ref, g_ref, raw_ref, qg_ref, kg_ref, cos_ref, sin_ref,
        gq_ref, gkv_ref, gain_ref, key_sum, value_sum, q_terms,
    ):
        step = pl.program_id(0)

        @pl.when(step == 0)
        def _():
            key_sum[...] = jnp.zeros_like(key_sum)
            value_sum[...] = jnp.zeros_like(value_sum)
            q_terms[...] = jnp.zeros_like(q_terms)

        def block(index):
            start = index * rows
            for kv_head in range(kv_heads):
                at = slice(kv_head * head_dim, (kv_head + 1) * head_dim)
                queries = stack_heads(q_ref[...], kv_head, heads_per, head_dim)
                heads = stack_heads(g_ref[...], kv_head, heads_per, head_dim)
                logs_at = log_ref[kv_head][:, :1]
                parts = [(start, start + rows)]
                if index:
                    parts.append((0, start))
                probs = []
                moved = []
                inner = 0.0
                for low, high in parts:
                    scores = cols_product(queries, k_ref[low:high, at])
                    if low == start:
                        scores = causal(scores, rows)
                    prob = jnp.exp(scores - logs_at)
                    value_sum[low:high, at] += rows_product(prob.astype(BF16), heads)
                    grad_prob = cols_product(heads, v_ref[low:high, at])
                    inner = inner + jnp.sum(prob * grad_prob, axis=1, keepdims=True)
                    probs.append(prob)
                    moved.append(grad_prob)
                grad_query = 0.0
                for (low, high), prob, grad_prob in zip(parts, probs, moved):
                    grad_scores = (prob * (grad_prob - inner)).astype(BF16)
                    grad_query = grad_query + plain_product(grad_scores, k_ref[low:high, at])
                    key_sum[low:high, at] += rows_product(grad_scores, queries)
                cosine_block = cos_ref[start : start + rows]
                sine_block = sin_ref[start : start + rows]
                for h in range(heads_per):
                    spot = (kv_head * heads_per + h) * head_dim
                    piece = turn(
                        grad_query[h * rows : (h + 1) * rows] * scale, cosine_block, -sine_block
                    )
                    back, terms = head_back(
                        raw_ref[start : start + rows, spot : spot + head_dim], qg_ref[...], piece
                    )
                    gq_ref[:, spot : spot + head_dim] = back.astype(BF16)
                    q_terms[...] += terms

        for index in range(count):
            pl.when(step == index)(lambda index=index: block(index))

        @pl.when(step == count - 1)
        def _():
            k_terms = jnp.zeros((1, head_dim), F32)
            for kv_head in range(kv_heads):
                at = slice(kv_head * head_dim, (kv_head + 1) * head_dim)
                piece = turn(key_sum[:, at], cos_ref[...], -sin_ref[...])
                spot = q_cols + kv_head * head_dim
                back, terms = head_back(raw_ref[:, spot : spot + head_dim], kg_ref[...], piece)
                k_terms = k_terms + terms
                back = back.astype(BF16)
                for index in range(count):
                    here = pl.ds(pl.multiple_of((index ^ spots_ref[0]) * rows, rows), rows)
                    gkv_ref[here, at] = back[index * rows : (index + 1) * rows]
            for index in range(count):
                here = pl.ds(pl.multiple_of((index ^ spots_ref[0]) * rows, rows), rows)
                gkv_ref[here, k_cols:] = value_sum[index * rows : (index + 1) * rows].astype(BF16)
            gain_ref[0:1] = q_terms[...]
            gain_ref[1:2] = k_terms
            gain_ref[2:] = jnp.zeros((6, head_dim), F32)

    def slot(i, spots):
        return (i ^ spots[0], 0)

    return call(
        kernel,
        (count,),
        [
            pl.BlockSpec((rows, q_cols), lambda i, spots: (i, 0)),
            whole((group_rows, k_cols)),
            whole((group_rows, k_cols)),
            pl.BlockSpec((kv_heads, heads_per * rows, head_dim), lambda i, spots: (0, i, 0)),
            pl.BlockSpec((rows, q_cols), slot),
            whole((group_rows, q_cols + k_cols)),
            whole((1, head_dim)),
            whole((1, head_dim)),
            whole((group_rows, head_dim)),
            whole((group_rows, head_dim)),
        ],
        [
            pl.BlockSpec((rows, q_cols), slot),
            whole((group_rows, 2 * k_cols)),
            whole((8, head_dim)),
        ],
        [
            jax.ShapeDtypeStruct((group_rows, q_cols), BF16),
            jax.ShapeDtypeStruct((group_rows, 2 * k_cols), BF16),
            jax.ShapeDtypeStruct((8, head_dim), F32),
        ],
        [
            pltpu.VMEM((group_rows, k_cols), F32),
            pltpu.VMEM((group_rows, k_cols), F32),
            pltpu.VMEM((1, head_dim), F32),
        ],
        10 * group_rows * group_rows * q_cols,
        group_rows * q_cols * 16,
        spots, query, key, value, logs, grads, raw, q_gain, k_gain, cosine, sine,
    )


def gated_units(spots, mine, mate, w_gate, gate_mate, w_up, up_mate, grad_hidden):
    group_rows, width_local = mine.shape
    units = gate_mate.shape[1]
    count = lax.axis_size("col")
    rows = group_rows // count

    def kernel(
        spots_ref, mine_ref, mate_ref, wg_ref, wgm_ref, wu_ref, wum_ref, gh_ref,
        hidden_ref, gg_ref, gu_ref,
    ):
        left, right = mine_ref[...], mate_ref[...]
        gate = plain_product(left, wg_ref[...]) + plain_product(right, wgm_ref[...])
        up = plain_product(left, wu_ref[...]) + plain_product(right, wum_ref[...])
        sigm = jax.nn.sigmoid(gate)
        silu = gate * sigm
        grad = gh_ref[...]
        hidden_ref[...] = (silu * up).astype(BF16)
        gg_ref[...] = (grad * up * sigm * (1.0 + gate * (1.0 - sigm))).astype(BF16)
        gu_ref[...] = (grad * silu).astype(BF16)

    def straight(i, spots):
        return (i, 0)

    def own(i, spots):
        return (0, spots[1])

    return call(
        kernel,
        (count,),
        [
            pl.BlockSpec((rows, width_local), straight),
            pl.BlockSpec((rows, width_local), straight),
            pl.BlockSpec((width_local, units), own),
            whole((width_local, units)),
            pl.BlockSpec((width_local, units), own),
            whole((width_local, units)),
            pl.BlockSpec((rows, units), straight),
        ],
        [pl.BlockSpec((rows, units), straight)] * 3,
        [jax.ShapeDtypeStruct((group_rows, units), BF16)] * 3,
        [],
        8 * group_rows * width_local * units,
        group_rows * width_local * 4 + width_local * units * 8 + group_rows * units * 10,
        spots, mine, mate, w_gate, gate_mate, w_up, up_mate, grad_hidden,
    )


def rms_back(values, inverse, gain, grads, width):
    unit_vals = values * inverse
    scaled = grads * gain
    inner = row_sum(jnp.sum(scaled * unit_vals, axis=1)) / width
    return (inverse * (scaled - unit_vals * inner[:, None]), jnp.sum(grads * unit_vals, axis=0))


def on_device(
    tokens,
    norm1_gain,
    w_q,
    w_k,
    w_v,
    q_gain,
    k_gain,
    w_o,
    norm2_gain,
    w_gate,
    w_up,
    w_down,
    grad_out,
):
    me = lax.axis_index("row")
    mate = 1 - me
    width_local = tokens.shape[1]
    width = width_local * lax.axis_size("row")
    gain_one = take(norm1_gain, me, width_local, 0)
    gain_one_mate = take(norm1_gain, mate, width_local, 0)
    gain_two = take(norm2_gain, me, width_local, 0)
    head_dim = q_gain.shape[0]
    q_cols = w_q.shape[1] // 2
    k_cols = w_k.shape[1] // 2
    units = w_gate.shape[1] // 2

    tokens_mine = jnp.concatenate(gather_tokens(tokens), axis=0)
    tokens_mate = row_swap(tokens_mine)

    qkv_mine = jnp.concatenate(
        [take(w_q, me, q_cols, 1), take(w_k, me, k_cols, 1), take(w_v, me, k_cols, 1)], axis=1
    )
    qkv_away = jnp.concatenate(
        [take(w_q, mate, q_cols, 1), take(w_k, mate, k_cols, 1), take(w_v, mate, k_cols, 1)],
        axis=1,
    )
    qkv_mate = row_swap(qkv_away)
    gate_mine = take(w_gate, me, units, 1)
    gate_away = take(w_gate, mate, units, 1)
    gate_mate = row_swap(gate_away)
    up_mine = take(w_up, me, units, 1)
    up_away = take(w_up, mate, units, 1)
    up_mate = row_swap(up_away)
    down_mine = take(w_down, me, units, 0)
    down_away = take(w_down, mate, units, 0)
    down_mate = row_swap(down_away)

    here = lax.axis_index("col") if lax.axis_size("col") == 4 else 0 * me
    spots = jnp.stack([here, me]).astype(jnp.int32)
    cosine, sine = rope_tables(SEQ_LEN, head_dim)
    q_gain = q_gain[None, :]
    k_gain = k_gain[None, :]
    normed_mine, raw, query_rot, key_rot, value_low = project_qkv(
        spots, tokens_mine, tokens_mate, gain_one[None, :], gain_one_mate[None, :],
        qkv_mine, qkv_mate, q_gain, k_gain, cosine, sine,
    )
    grads_blocks, raw = gather_tokens(grad_out, raw)
    grads_mine = jnp.concatenate(grads_blocks, axis=0)
    heads_mine, logs = attend(spots, query_rot, key_rot, value_low, head_dim)
    heads_mate = row_swap(heads_mine)
    o_mine = take(w_o, me, q_cols, 0)
    o_away = take(w_o, mate, q_cols, 0)
    attn_out = scatter_tokens(plain_product(heads_mine, o_mine) + plain_product(heads_mate, o_away))
    inputs = tokens.astype(F32)
    mid = inputs + attn_out
    inverse_two = lax.rsqrt(row_sum(jnp.sum(mid * mid, axis=1)) / width + EPS)[:, None]
    normed_two = (mid * inverse_two * gain_two).astype(BF16)
    two_mine = jnp.concatenate(gather_tokens(normed_two), axis=0)
    two_mate = row_swap(two_mine)

    grads_mate = row_swap(grads_mine)
    grad_hidden = cols_product(grads_mine, down_mine) + cols_product(grads_mate, down_mate)

    hidden_mine, grad_gate, grad_up = gated_units(
        spots, two_mine, two_mate, w_gate, gate_mate, w_up, up_mate, grad_hidden
    )
    hidden_mate = row_swap(hidden_mine)
    grad_gate_mate = row_swap(grad_gate)
    grad_up_mate = row_swap(grad_up)

    sums = LineSums()

    def weight_grad(kind, index, left, right, pieces=1):
        part = rows_product(left, right).astype(BF16)
        if pieces == 1:
            sums.add(kind + str(index), part)
            return
        size = part.shape[0] // pieces
        parts = lax.optimization_barrier(
            tuple(part[piece * size : (piece + 1) * size] for piece in range(pieces))
        )
        for piece in range(pieces):
            sums.add(kind + str(index + piece), parts[piece])

    weight_grad("d", 0, hidden_mine, grads_mine, 2)
    weight_grad("g", 0, two_mine, grad_gate, 2)
    weight_grad("u", 0, two_mine, grad_up, 2)
    weight_grad("d", 2, hidden_mate, grads_mine, 2)
    weight_grad("g", 2, two_mine, grad_gate_mate, 2)
    weight_grad("u", 2, two_mine, grad_up_mate, 2)

    grad_two_part = (
        cols_product(grad_gate, gate_mine)
        + cols_product(grad_up, up_mine)
        + cols_product(grad_gate_mate, gate_away)
        + cols_product(grad_up_mate, up_away)
    )
    grad_normed_two = scatter_tokens(grad_two_part)
    grad_mid_norm, gain_two_part = rms_back(mid, inverse_two, gain_two, grad_normed_two, width)
    grad_mid = grad_out.astype(F32) + grad_mid_norm
    grad_mid_low = grad_mid.astype(BF16)
    attn_mine = jnp.concatenate(gather_tokens(grad_mid_low), axis=0)
    weight_grad("o", 0, heads_mine, attn_mine)
    weight_grad("o", 1, heads_mate, attn_mine)
    grad_heads = (
        cols_product(attn_mine, o_mine) + row_swap(cols_product(attn_mine, o_away))
    ).astype(BF16)

    grad_query, grad_kv, head_gains = attend_back(
        spots, query_rot, key_rot, value_low, logs, grad_heads, raw, q_gain, k_gain, cosine, sine
    )
    grad_qkv = jnp.concatenate([grad_query, grad_kv], axis=1)
    grad_qkv_mate = row_swap(grad_qkv)
    weight_grad("q", 0, normed_mine, grad_qkv[:, :q_cols])
    weight_grad("q", 1, normed_mine, grad_qkv_mate[:, :q_cols])
    weight_grad("v", 0, normed_mine, grad_qkv[:, q_cols:])
    weight_grad("v", 1, normed_mine, grad_qkv_mate[:, q_cols:])
    input_part = cols_product(grad_qkv, qkv_mine) + cols_product(grad_qkv_mate, qkv_away)
    grad_normed_one = scatter_tokens(input_part)
    late_mine, late_mate, grad_normed_one = lax.optimization_barrier(
        (hidden_mine, hidden_mate, grad_normed_one)
    )
    mlp_part = plain_product(late_mine, down_mine) + plain_product(late_mate, down_away)
    mlp_out = scatter_tokens(mlp_part)
    block_out = (mid + mlp_out).astype(BF16)
    inverse_one = lax.rsqrt(row_sum(jnp.sum(inputs * inputs, axis=1)) / width + EPS)[:, None]
    grad_input_norm, gain_one_part = rms_back(inputs, inverse_one, gain_one, grad_normed_one, width)
    grad_tokens = grad_mid + grad_input_norm

    gains = [
        lax.dynamic_update_slice_in_dim(
            jnp.zeros((width,), F32), part, me * width_local, 0
        )
        for part in (gain_one_part, gain_two_part)
    ]
    gains.append(head_gains[0])
    gains.append(head_gains[1])
    gain_sum = row_sum(jnp.concatenate(gains))
    if lax.axis_size("col") == 4:
        gain_sum = gain_sum + xor_hop(gain_sum, 1)
        gain_sum = gain_sum + xor_hop(gain_sum, 2)
    else:
        gain_sum = lax.psum(gain_sum, "col")
    sums.add("n0", gain_sum)
    total = sums.totals
    gain_sum = total["n0"]
    grad_norm1 = gain_sum[:width]
    grad_norm2 = gain_sum[width : 2 * width]
    grad_q_gain = gain_sum[2 * width : 2 * width + head_dim]
    grad_k_gain = gain_sum[2 * width + head_dim :]

    def place(firsts, seconds, axis):
        rows = firsts[0].shape[0]
        span = rows * len(firsts) if axis == 0 else firsts[0].shape[1]
        shape = [rows * len(firsts), firsts[0].shape[1]]
        shape[axis] *= 2
        whole = jnp.zeros(shape, F32)
        for owner, parts in ((me, firsts), (mate, seconds)):
            for index, part in enumerate(parts):
                start = [index * rows, 0]
                start[axis] = start[axis] + owner * span
                whole = lax.dynamic_update_slice(whole, part.astype(F32), start)
        return whole

    def halves(kind):
        parts = [total[kind + str(index)] for index in range(4)]
        return (parts[:2], parts[2:])

    return (
        block_out,
        grad_tokens,
        grad_norm1,
        place([total["q0"]], [total["q1"]], 1),
        place([total["v0"][:, :k_cols]], [total["v1"][:, :k_cols]], 1),
        place([total["v0"][:, k_cols:]], [total["v1"][:, k_cols:]], 1),
        grad_q_gain,
        grad_k_gain,
        place([total["o0"]], [total["o1"]], 0),
        grad_norm2,
        place(*halves("g"), 1),
        place(*halves("u"), 1),
        place(*halves("d"), 0),
    )


def solution(mesh):
    return jax.shard_map(
        on_device,
        mesh=mesh,
        in_specs=(
            P(("dp", "col"), "row"),
            P(),
            P("row", "col"),
            P("row", "col"),
            P("row", "col"),
            P(),
            P(),
            P("col", "row"),
            P(),
            P("row", "col"),
            P("row", "col"),
            P("col", "row"),
            P(("dp", "col"), "row"),
        ),
        out_specs=(
            P(("dp", "col"), "row"),
            P(("dp", "col"), "row"),
            P(),
            P("row", "col"),
            P("row", "col"),
            P("row", "col"),
            P(),
            P(),
            P("col", "row"),
            P(),
            P("row", "col"),
            P("row", "col"),
            P("col", "row"),
        ),
        check_vma=False,
    )
```
